32 devices in a mesh: blk: 4 (over y, x), ep: 8 (over z, core).
Axes of the slice: x: 2, y: 2, z: 4, core: 2. Of those that a mesh axis runs over, the one named last changes fastest.
Arguments:
- tokens: bfloat16 [4096, 1024], P(('blk', 'ep')), may hold values from -6 to 6
- expert_ids: int32 [4096, 6], P(('blk', 'ep')), may hold values from 0 to 63, all different within a row; in each aligned block of 128 rows (0 to 127, 128 to 255, ...) at most 16 rows name the same one
- route_weight: float32 [4096, 6], P(('blk', 'ep')), may hold values from 0.05 to 1
- gate_weight: bfloat16 [1024, 64, 768], P('blk', 'ep'), may hold values from -0.1875 to 0.1875
- up_weight: bfloat16 [1024, 64, 768], P('blk', 'ep'), may hold values from -0.1875 to 0.1875
- down_weight: bfloat16 [1024, 64, 768], P('blk', 'ep'), may hold values from -0.21875 to 0.21875
- out_grad: bfloat16 [4096, 1024], P(('blk', 'ep')), may hold values from -6 to 6
Outputs:
- layer_output: bfloat16 [4096, 1024], P(('blk', 'ep'))
- grad_tokens: float32 [4096, 1024], P(('blk', 'ep'))
- grad_route: float32 [4096, 6], P(('blk', 'ep'))
- grad_gate: float32 [1024, 64, 768], P('blk', 'ep')
- grad_up: float32 [1024, 64, 768], P('blk', 'ep')
- grad_down: float32 [1024, 64, 768], P('blk', 'ep')
The draws below stay inside these ranges and needn't reach their ends.
Inputs may be any that keep to these rules, and one draw needn't show every extreme that they name: `expert_ids`: within the 128 tokens of one device, the 6 experts of a token differ, and no expert is named by more than 16 of them; in every draw some expert is named by exactly 16 tokens of some device.
All inputs are finite; a program needn't handle non-finite values.
Results may differ from the reference program's by a relative error of at most 0.008.
Values may be sent and summed in bfloat16 or wider, within the bound.
No kernel may reach another device: no remote copies, remote signals or barrier semaphores. Data moves between devices by JAX's collectives and lax.ppermute only.
A program may use at most 256 MiB of HBM per device.

```python
import math
import jax
import jax.numpy as jnp
import numpy as np
from jax import lax

D = 1024
FF = 768
EXPERTS = 64
TOP = 6
TOK_DEV = 128
CAP = 16
TOKENS = 4096
N_BLK = 4
N_EP = 8


def shard_levels(rng, extent, shards, low, top_value):
    def one(dim, parts):
        heights = jax.random.uniform(jax.random.fold_in(jax.random.fold_in(rng, 6), dim), (parts,), jnp.float32, low / len(shards), top_value / len(shards))
        return jnp.repeat(jnp.exp(heights), extent[dim] // parts).reshape((-1,) + (1,) * (len(extent) - dim - 1))

    factor_of = one(*shards[0])
    for cut in shards[1:]:
        factor_of = factor_of * one(*cut)
    return factor_of


def routed_block(own_key, own, number, rows, number_of, top, reach, lean):
    order = jax.random.permutation(own_key, number_of)
    heavy_load, ordinary = shares(number_of, rows * top, reach, lean, True), shares(number_of, rows * top, reach, lean, False)
    places = jnp.arange(number_of)

    def named(lengths, offset_by):
        used = int((lengths > 0).sum())
        fixed = max(1, used // 4)
        passed = fixed + (places - fixed + offset_by * (used - fixed)) % max(1, number_of - fixed)
        return jnp.zeros((number_of,), jnp.int32).at[order[jnp.where(places < fixed, places, passed)]].set(jnp.asarray(lengths, jnp.int32))

    lengths = jnp.where(number % 4 == 0, named(heavy_load, number // 4), named(ordinary, number - number // 4 - 1))
    mixed = jax.random.permutation(jax.random.fold_in(own, 3), number_of)
    donor, sink = mixed[0:number_of // 2 * 2:2], mixed[1:number_of // 2 * 2:2]
    slack = jnp.minimum(lengths[donor] - 1, reach - lengths[sink]) // 2
    slack = jnp.where((donor == order[0]) | (sink == order[0]) | (lengths[sink] == 0), 0, jnp.maximum(slack, 0))
    passed = jax.random.randint(jax.random.fold_in(own, 4), (number_of // 2,), 0, 1 << 20) % (slack + 1)
    lengths = lengths.at[donor].add(-passed).at[sink].add(passed)
    labels = jnp.searchsorted(jnp.cumsum(lengths), jnp.arange(rows * top), side="right").astype(jnp.int32)
    listing = labels.reshape(top, rows).T
    listing = listing[jax.random.permutation(jax.random.fold_in(own, 1), rows)]
    offset_by = jax.random.randint(jax.random.fold_in(own, 2), (rows, 1), 0, top)
    return jnp.take_along_axis(listing, (jnp.arange(top)[None, :] + offset_by) % top, axis=1)


def shares(number_of, total, reach, slope, full):
    loads = [(1 << 20) // math.isqrt(standing ** slope) + 1 for standing in range(1, number_of + 1)]
    largest = reach if full else min(reach, max(-(-total // number_of), total * loads[0] // sum(loads)))
    least = 1 if total - largest >= number_of - 1 else 0
    counts, rest = [largest] + [least] * (number_of - 1), total - largest - least * (number_of - 1)
    while rest > 0:
        movable = [i for i in range(1, number_of) if counts[i] < largest] or [i for i in range(1, number_of) if counts[i] < reach]
        whole, left = sum([loads[i] for i in movable]), rest
        for i in movable:
            more = min(reach - counts[i], max(1, left * loads[i] // whole), rest)
            counts[i] = counts[i] + more
            rest = rest - more
    return np.array(counts)


def bell_draw(key, extent, spread, reach, pieces=(), kind=jnp.bfloat16):
    drawn = spread * jax.random.normal(key, extent, jnp.float32)
    if pieces:
        drawn = drawn * shard_levels(key, extent, pieces, -0.22, 0.18)
    return jnp.clip(drawn, -reach, reach).astype(kind)


def setup_inputs(seed: int = 0) -> dict:
    seeds = jax.random.split(jax.random.key(seed), 8)
    tokens = bell_draw(seeds[0], (TOKENS, D), 1.0, 6.0, ((0, 32),))
    expert_ids_keys = jax.random.split(jax.random.fold_in(seeds[1], 1), TOKENS // TOK_DEV)
    expert_ids_turns = jax.random.permutation(jax.random.fold_in(seeds[1], 3), TOKENS // TOK_DEV)
    expert_ids = jax.vmap(lambda own, number: routed_block(jax.random.fold_in(seeds[1], 2), own, number, TOK_DEV, EXPERTS, TOP, CAP, 2))(expert_ids_keys, expert_ids_turns).reshape((TOKENS, TOP))
    route_weight = jnp.clip(jnp.exp(math.log(1.0) - 2.9957323 * jax.random.uniform(seeds[2], (TOKENS, TOP), jnp.float32) ** shard_levels(seeds[2], (TOKENS, TOP), ((0, 32),), -0.2, 0.2)), 0.05, 1.0)
    gate_weight = bell_draw(seeds[3], (D, EXPERTS, FF), D ** -0.5, 0.1875, ((0, 4), (1, 8)))
    up_weight = bell_draw(seeds[4], (D, EXPERTS, FF), D ** -0.5, 0.1875, ((0, 4), (1, 8)))
    down_weight = bell_draw(seeds[5], (D, EXPERTS, FF), FF ** -0.5, 0.21875, ((0, 4), (1, 8)))
    out_grad = bell_draw(seeds[6], (TOKENS, D), 1.0, 6.0, ((0, 32),))
    return dict(tokens=tokens, expert_ids=expert_ids, route_weight=route_weight, gate_weight=gate_weight, up_weight=up_weight, down_weight=down_weight, out_grad=out_grad)


def rounded(tensor):
    return lax.optimization_barrier(tensor.astype(jnp.bfloat16)).astype(jnp.float32)


def reference(tokens, expert_ids, route_weight, gate_weight, up_weight, down_weight, out_grad):
    devices = N_BLK * N_EP
    pair_count = TOK_DEV * TOP
    model_width = tokens.shape[1]
    id_rows = expert_ids.reshape(devices, pair_count)
    onehot = (id_rows[:, :, None] == jnp.arange(EXPERTS, dtype=jnp.int32)[None, None, :]).astype(jnp.int32)
    slot_rank = jnp.sum((jnp.cumsum(onehot, axis=1) - 1) * onehot, axis=2)
    device_row = jnp.arange(devices, dtype=jnp.int32)[:, None]
    position = (id_rows * devices + device_row) * CAP + slot_rank
    pair_index = jnp.arange(devices * pair_count, dtype=jnp.int32)
    slot_table = jnp.full((EXPERTS * devices * CAP,), -1, dtype=jnp.int32)
    slot_table = slot_table.at[position.reshape(-1)].set(pair_index).reshape(EXPERTS, N_BLK, N_EP * CAP)
    weight_flat = route_weight.reshape(-1).astype(jnp.float32)
    grad_rows = out_grad.astype(jnp.float32)

    def one_expert(running, per_expert):
        mixed_acc, token_acc, route_acc = running
        pair_ids, w_gate, w_up, w_down = per_expert
        w_gate = w_gate.astype(jnp.float32)
        w_up = w_up.astype(jnp.float32)
        w_down = w_down.astype(jnp.float32)
        live_rows = pair_ids >= 0
        safe_ids = jnp.where(live_rows, pair_ids, 0)
        token_ids = safe_ids // TOP
        routed_rows = jnp.where(live_rows[:, :, None], tokens[token_ids].astype(jnp.float32), 0.0)
        pair_weight = jnp.where(live_rows, weight_flat[safe_ids], 0.0)
        gate_pre = jnp.einsum("brd,df->brf", routed_rows, w_gate)
        up_pre = jnp.einsum("brd,df->brf", routed_rows, w_up)
        gate_sig = jax.nn.sigmoid(gate_pre)
        hidden = rounded(gate_pre * gate_sig * up_pre)
        expert_out = rounded(jnp.einsum("brf,df->brd", hidden, w_down))
        token_grad = jnp.where(live_rows[:, :, None], grad_rows[token_ids], 0.0)
        flat_tokens = token_ids.reshape(-1)
        mixed_acc = mixed_acc.at[flat_tokens].add((pair_weight[:, :, None] * expert_out).reshape(-1, model_width))
        route_val = jnp.sum(expert_out * token_grad, axis=2)
        route_target = jnp.where(live_rows, pair_ids, devices * pair_count)
        route_acc = route_acc.at[route_target.reshape(-1)].set(route_val.reshape(-1), mode="drop")
        slot_grad = rounded(pair_weight[:, :, None] * token_grad)
        grad_hidden = jnp.einsum("brd,df->brf", slot_grad, w_down)
        gate_delta = rounded(grad_hidden * up_pre * gate_sig * (1.0 + gate_pre * (1.0 - gate_sig)))
        up_delta = rounded(grad_hidden * gate_pre * gate_sig)
        input_grad = rounded(jnp.einsum("brf,df->brd", gate_delta, w_gate) + jnp.einsum("brf,df->brd", up_delta, w_up))
        token_acc = token_acc.at[flat_tokens].add(input_grad.reshape(-1, model_width))
        part_gate = rounded(jnp.einsum("brd,brf->bdf", routed_rows, gate_delta))
        part_up = rounded(jnp.einsum("brd,brf->bdf", routed_rows, up_delta))
        part_down = rounded(jnp.einsum("brd,brf->bdf", slot_grad, hidden))
        sums = (jnp.sum(part_gate, axis=0), jnp.sum(part_up, axis=0), jnp.sum(part_down, axis=0))
        return (mixed_acc, token_acc, route_acc), sums

    initial = (jnp.zeros((TOKENS, model_width), jnp.float32), jnp.zeros((TOKENS, model_width), jnp.float32), jnp.zeros((TOKENS * TOP,), jnp.float32))
    per_expert = (slot_table, jnp.moveaxis(gate_weight, 1, 0), jnp.moveaxis(up_weight, 1, 0), jnp.moveaxis(down_weight, 1, 0))
    finals, grads = lax.scan(one_expert, initial, per_expert)
    mixed_acc, token_acc, route_acc = finals
    grad_gate = jnp.moveaxis(grads[0], 0, 1)
    grad_up = jnp.moveaxis(grads[1], 0, 1)
    grad_down = jnp.moveaxis(grads[2], 0, 1)
    return (mixed_acc.astype(jnp.bfloat16), token_acc, route_acc.reshape(TOKENS, TOP), grad_gate, grad_up, grad_down)
```

```python
import jax
import jax.numpy as jnp
from jax import lax
from jax.sharding import PartitionSpec as P

EXPERTS = 64
CAP = 16
BF = jnp.bfloat16
F32 = jnp.float32


def dot(a, b, ca, cb):
    return lax.dot_general(a, b, (((ca,), (cb,)), ((), ())), preferred_element_type=F32)


def expand_rows(routed, weights):
    return jnp.einsum("erd,def->erf", routed, weights, preferred_element_type=jnp.float32)


def contract_rows(inner, weights):
    return jnp.einsum("erf,def->erd", inner, weights, preferred_element_type=jnp.float32)


def outer_rows(routed, inner):
    return jnp.einsum("erd,erf->def", routed, inner, preferred_element_type=jnp.float32)


def gathered_body(tokens, expert_ids, route_weight, gate_weight, up_weight, down_weight, out_grad):
    tok_count, model_width = tokens.shape
    top_count = expert_ids.shape[1]
    experts = EXPERTS
    capacity = CAP
    flat_ids = expert_ids.reshape(-1)
    onehot = (flat_ids[:, None] == jnp.arange(experts, dtype=jnp.int32)[None, :]).astype(jnp.int32)
    slot_rank = jnp.sum((jnp.cumsum(onehot, axis=0) - 1) * onehot, axis=1)
    target = flat_ids * capacity + slot_rank
    repeated = jnp.repeat(tokens, top_count, axis=0)
    outgoing = jnp.zeros((experts * capacity, model_width), jnp.bfloat16).at[target].set(repeated)
    received = lax.all_to_all(
        outgoing.reshape(experts, capacity, model_width),
        "ep",
        split_axis=0,
        concat_axis=1,
        tiled=True,
    )
    gate_full, up_full, down_full = (
        lax.all_gather(gate_weight, "blk", axis=0, tiled=True),
        lax.all_gather(up_weight, "blk", axis=0, tiled=True),
        lax.all_gather(down_weight, "blk", axis=0, tiled=True),
    )
    gate_pre = expand_rows(received, gate_full)
    up_pre = expand_rows(received, up_full)
    gate_sig = jax.nn.sigmoid(gate_pre)
    hidden = (gate_pre * gate_sig * up_pre).astype(jnp.bfloat16)
    expert_out = contract_rows(hidden, down_full).astype(jnp.bfloat16)
    returned = lax.all_to_all(expert_out, "ep", split_axis=1, concat_axis=0, tiled=True)
    chosen = returned.reshape(experts * capacity, model_width)[target].reshape(
        tok_count, top_count, model_width
    )
    chosen_f32 = chosen.astype(jnp.float32)
    layer_output = jnp.sum(route_weight[:, :, None] * chosen_f32, axis=1).astype(jnp.bfloat16)
    grad_f32 = out_grad.astype(jnp.float32)
    grad_route = jnp.sum(chosen_f32 * grad_f32[:, None, :], axis=2)
    slot_grad = (route_weight[:, :, None] * grad_f32[:, None, :]).astype(jnp.bfloat16)
    grad_send = (
        jnp.zeros((experts * capacity, model_width), jnp.bfloat16)
        .at[target]
        .set(slot_grad.reshape(-1, model_width))
    )
    grad_recv = lax.all_to_all(
        grad_send.reshape(experts, capacity, model_width),
        "ep",
        split_axis=0,
        concat_axis=1,
        tiled=True,
    )
    down_summed = lax.psum_scatter(
        outer_rows(grad_recv, hidden).astype(jnp.bfloat16), "blk", scatter_dimension=0, tiled=True
    ).astype(jnp.float32)
    grad_hidden = expand_rows(grad_recv, down_full)
    gate_delta = (grad_hidden * up_pre * gate_sig * (1.0 + gate_pre * (1.0 - gate_sig))).astype(
        jnp.bfloat16
    )
    up_delta = (grad_hidden * gate_pre * gate_sig).astype(jnp.bfloat16)
    input_grad = (contract_rows(gate_delta, gate_full) + contract_rows(up_delta, up_full)).astype(
        jnp.bfloat16
    )
    grad_back = lax.all_to_all(input_grad, "ep", split_axis=1, concat_axis=0, tiled=True)
    picked_grad = grad_back.reshape(experts * capacity, model_width)[target].reshape(
        tok_count, top_count, model_width
    )
    grad_tokens = jnp.sum(picked_grad.astype(jnp.float32), axis=1)
    pair_summed = lax.psum_scatter(
        jnp.stack(
            [outer_rows(received, gate_delta), outer_rows(received, up_delta)], axis=1
        ).astype(jnp.bfloat16),
        "blk",
        scatter_dimension=0,
        tiled=True,
    ).astype(jnp.float32)
    grad_gate = pair_summed[:, 0]
    grad_up = pair_summed[:, 1]
    return (layer_output, grad_tokens, grad_route, grad_gate, grad_up, down_summed)


def expert_body(tokens, expert_ids, route_weight, gate_weight, up_weight, down_weight, out_grad):
    nb, ne = lax.axis_size("blk"), lax.axis_size("ep")
    me = lax.axis_index("blk")
    tok, width = tokens.shape
    top = expert_ids.shape[1]
    local_experts = gate_weight.shape[1]
    own = local_experts // nb
    chunk = gate_weight.shape[0]
    inner = gate_weight.shape[2]

    def hop(x, j):
        return lax.ppermute(x, "blk", [(i, i ^ j) for i in range(nb)])

    def spread(x):
        return [x] + [hop(x, j) for j in range(1, nb)]

    def to_local(x):
        return jnp.concatenate(
            [lax.dynamic_slice_in_dim(x, (me ^ j) * chunk, chunk, 1) for j in range(nb)], axis=1
        )

    ids_all = jnp.concatenate(spread(expert_ids), 0)
    rw_all = jnp.concatenate(spread(route_weight), 0)
    tok_all = to_local(jnp.concatenate(spread(tokens), 0))
    og_all = to_local(jnp.concatenate(spread(out_grad), 0))

    w_emajor = [jnp.swapaxes(w, 0, 1) for w in (gate_weight, up_weight, down_weight)]

    def weight_of(w, i):
        pieces = []
        for j in range(nb):
            piece = lax.dynamic_index_in_dim(w, (me ^ j) * own + i, 0, keepdims=False)
            pieces.append(piece if j == 0 else hop(piece, j))
        return jnp.concatenate(pieces, 0)

    weights = [[weight_of(w, i) for w in w_emajor] for i in range(own)]

    rows = nb * tok
    row = jnp.arange(rows)
    before = ((row[:, None] > row[None, :]) & (row[:, None] // tok == row[None, :] // tok)).astype(BF)
    slots = ne * nb * CAP
    slot = jnp.arange(slots)
    slot_dest, slot_group, slot_rank = slot // (nb * CAP), (slot // CAP) % nb, slot % CAP

    sel, sel_w, gates = [], [], []
    for i in range(own):
        experts = jnp.arange(ne) * local_experts + me * own + i
        eq = ids_all[:, :, None] == experts[None, None, :]
        member = jnp.any(eq, axis=1)
        weight = jnp.sum(jnp.where(eq, rw_all[:, :, None], 0.0), axis=1)
        rank = dot(before, member.astype(BF), 1, 0)
        rank = jnp.where(member, rank, -1.0).astype(jnp.int32)
        rank_s = jnp.repeat(rank.T, nb * CAP, axis=0)
        weight_s = jnp.repeat(weight.T, nb * CAP, axis=0)
        hit = (rank_s == slot_rank[:, None]) & (slot_group[:, None] == row[None, :] // tok)
        sel.append(hit.astype(BF))
        sel_w.append(jnp.where(hit, weight_s, 0.0))
        gates.append(eq)

    def exchange(x):
        return lax.all_to_all(
            x.reshape(ne, nb * CAP, width), "ep", split_axis=0, concat_axis=0, tiled=True
        ).reshape(slots, width)

    routed, graded = [], []
    for i in range(own):
        routed.append(exchange(dot(sel[i], tok_all, 1, 0).astype(BF)))
        slot_grad = dot(sel[i], og_all, 1, 0) * jnp.sum(sel_w[i], axis=1, keepdims=True)
        graded.append(exchange(slot_grad.astype(BF)))

    outs, backs, grads = [], [], []
    for i in range(own):
        wg, wu, wd = weights[i]
        x, sg = routed[i], graded[i]
        gate_pre, up_pre = dot(x, wg, 1, 0), dot(x, wu, 1, 0)
        sig = jax.nn.sigmoid(gate_pre)
        hidden = (gate_pre * sig * up_pre).astype(BF)
        outs.append(exchange(dot(hidden, wd, 1, 1).astype(BF)))
        gh = dot(sg, wd, 1, 0)
        gate_delta = (gh * up_pre * sig * (1.0 + gate_pre * (1.0 - sig))).astype(BF)
        up_delta = (gh * gate_pre * sig).astype(BF)
        ig = dot(gate_delta, wg, 1, 1) + dot(up_delta, wu, 1, 1)
        backs.append(exchange(ig.astype(BF)))
        parts = (dot(x, gate_delta, 0, 0), dot(x, up_delta, 0, 0), dot(sg, hidden, 0, 0))
        got = []
        for part in parts:
            part = part.astype(BF).reshape(nb, chunk, inner)
            got.append([part[0]] + [hop(part[j], j) for j in range(1, nb)])
        grads.append(got)

    mixed = jnp.zeros((rows, width), F32)
    token_grad = jnp.zeros((rows, width), F32)
    route_grad = jnp.zeros((rows, top), F32)
    for i in range(own):
        high = sel_w[i].astype(BF)
        low = (sel_w[i] - high.astype(F32)).astype(BF)
        mixed += dot(high, outs[i], 0, 0) + dot(low, outs[i], 0, 0)
        token_grad += dot(sel[i], backs[i], 0, 0)
        score = dot(outs[i], og_all, 1, 1)
        score = jnp.where(sel[i] > 0, score, 0.0).reshape(ne, nb * CAP, rows).sum(1)
        route_grad += jnp.sum(jnp.where(gates[i], score.T[:, None, :], 0.0), axis=2)

    def from_local(x):
        out = []
        for c in range(nb):
            out.append(lax.dynamic_slice_in_dim(x, (me ^ c) * chunk, chunk, 1))
        return jnp.concatenate(out, 1)

    def gather_back(x):
        x = x.reshape((nb, tok) + x.shape[1:])
        total = x[0].astype(F32)
        for j in range(1, nb):
            total += hop(x[j], j).astype(F32)
        return total

    layer_output = gather_back(from_local(mixed).astype(BF)).astype(BF)
    grad_tokens = gather_back(from_local(token_grad).astype(BF))
    grad_route = gather_back(route_grad)

    def finish(m):
        order = jnp.stack([jnp.stack([grads[i][m][j] for i in range(own)], 0) for j in range(nb)], 0)
        buf = jnp.concatenate(
            [lax.dynamic_index_in_dim(order, me ^ j, 0, keepdims=False) for j in range(nb)], 0
        )
        return jnp.swapaxes(buf, 0, 1).astype(F32)

    return (layer_output, grad_tokens, grad_route, finish(0), finish(1), finish(2))


def solution(mesh):
    in_specs = (
        P(("blk", "ep"), None),
        P(("blk", "ep"), None),
        P(("blk", "ep"), None),
        P("blk", "ep", None),
        P("blk", "ep", None),
        P("blk", "ep", None),
        P(("blk", "ep"), None),
    )
    out_specs = (
        P(("blk", "ep"), None),
        P(("blk", "ep"), None),
        P(("blk", "ep"), None),
        P("blk", "ep", None),
        P("blk", "ep", None),
        P("blk", "ep", None),
    )
    nb, ne = mesh.shape["blk"], mesh.shape["ep"]
    whole_experts = nb & (nb - 1) == 0 and (EXPERTS // ne) % nb == 0
    body = expert_body if whole_experts else gathered_body
    return jax.shard_map(body, mesh=mesh, in_specs=in_specs, out_specs=out_specs, check_vma=False)
```

```python
import jax
import jax.numpy as jnp
from jax import lax
from jax.experimental import pallas as pl
from jax.experimental.pallas import tpu as pltpu
from jax.sharding import PartitionSpec as P

EXPERTS = 64
CAP = 16
BF = jnp.bfloat16
F32 = jnp.float32


def dot(a, b, ca, cb):
    return lax.dot_general(a, b, (((ca,), (cb,)), ((), ())), preferred_element_type=F32)


def expand_rows(routed, weights):
    return jnp.einsum("erd,def->erf", routed, weights, preferred_element_type=jnp.float32)


def contract_rows(inner, weights):
    return jnp.einsum("erf,def->erd", inner, weights, preferred_element_type=jnp.float32)


def outer_rows(routed, inner):
    return jnp.einsum("erd,erf->def", routed, inner, preferred_element_type=jnp.float32)


def gathered_body(tokens, expert_ids, route_weight, gate_weight, up_weight, down_weight, out_grad):
    tok_count, model_width = tokens.shape
    top_count = expert_ids.shape[1]
    experts = EXPERTS
    capacity = CAP
    flat_ids = expert_ids.reshape(-1)
    onehot = (flat_ids[:, None] == jnp.arange(experts, dtype=jnp.int32)[None, :]).astype(jnp.int32)
    slot_rank = jnp.sum((jnp.cumsum(onehot, axis=0) - 1) * onehot, axis=1)
    target = flat_ids * capacity + slot_rank
    repeated = jnp.repeat(tokens, top_count, axis=0)
    outgoing = jnp.zeros((experts * capacity, model_width), jnp.bfloat16).at[target].set(repeated)
    received = lax.all_to_all(
        outgoing.reshape(experts, capacity, model_width),
        "ep",
        split_axis=0,
        concat_axis=1,
        tiled=True,
    )
    gate_full, up_full, down_full = (
        lax.all_gather(gate_weight, "blk", axis=0, tiled=True),
        lax.all_gather(up_weight, "blk", axis=0, tiled=True),
        lax.all_gather(down_weight, "blk", axis=0, tiled=True),
    )
    gate_pre = expand_rows(received, gate_full)
    up_pre = expand_rows(received, up_full)
    gate_sig = jax.nn.sigmoid(gate_pre)
    hidden = (gate_pre * gate_sig * up_pre).astype(jnp.bfloat16)
    expert_out = contract_rows(hidden, down_full).astype(jnp.bfloat16)
    returned = lax.all_to_all(expert_out, "ep", split_axis=1, concat_axis=0, tiled=True)
    chosen = returned.reshape(experts * capacity, model_width)[target].reshape(
        tok_count, top_count, model_width
    )
    chosen_f32 = chosen.astype(jnp.float32)
    layer_output = jnp.sum(route_weight[:, :, None] * chosen_f32, axis=1).astype(jnp.bfloat16)
    grad_f32 = out_grad.astype(jnp.float32)
    grad_route = jnp.sum(chosen_f32 * grad_f32[:, None, :], axis=2)
    slot_grad = (route_weight[:, :, None] * grad_f32[:, None, :]).astype(jnp.bfloat16)
    grad_send = (
        jnp.zeros((experts * capacity, model_width), jnp.bfloat16)
        .at[target]
        .set(slot_grad.reshape(-1, model_width))
    )
    grad_recv = lax.all_to_all(
        grad_send.reshape(experts, capacity, model_width),
        "ep",
        split_axis=0,
        concat_axis=1,
        tiled=True,
    )
    down_summed = lax.psum_scatter(
        outer_rows(grad_recv, hidden).astype(jnp.bfloat16), "blk", scatter_dimension=0, tiled=True
    ).astype(jnp.float32)
    grad_hidden = expand_rows(grad_recv, down_full)
    gate_delta = (grad_hidden * up_pre * gate_sig * (1.0 + gate_pre * (1.0 - gate_sig))).astype(
        jnp.bfloat16
    )
    up_delta = (grad_hidden * gate_pre * gate_sig).astype(jnp.bfloat16)
    input_grad = (contract_rows(gate_delta, gate_full) + contract_rows(up_delta, up_full)).astype(
        jnp.bfloat16
    )
    grad_back = lax.all_to_all(input_grad, "ep", split_axis=1, concat_axis=0, tiled=True)
    picked_grad = grad_back.reshape(experts * capacity, model_width)[target].reshape(
        tok_count, top_count, model_width
    )
    grad_tokens = jnp.sum(picked_grad.astype(jnp.float32), axis=1)
    pair_summed = lax.psum_scatter(
        jnp.stack(
            [outer_rows(received, gate_delta), outer_rows(received, up_delta)], axis=1
        ).astype(jnp.bfloat16),
        "blk",
        scatter_dimension=0,
        tiled=True,
    ).astype(jnp.float32)
    grad_gate = pair_summed[:, 0]
    grad_up = pair_summed[:, 1]
    return (layer_output, grad_tokens, grad_route, grad_gate, grad_up, down_summed)


LIGHT, HEAVY = 1 << 10, 1 << 37


def call(kernel, name, grid, in_specs, out_specs, out_shape, scratch=(), cost=LIGHT):
    return pl.pallas_call(
        kernel,
        grid_spec=pltpu.PrefetchScalarGridSpec(
            num_scalar_prefetch=1,
            grid=grid,
            in_specs=in_specs,
            out_specs=out_specs,
            scratch_shapes=scratch,
        ),
        out_shape=out_shape,
        compiler_params=pltpu.CompilerParams(vmem_limit_bytes=48 << 20),
        cost_estimate=pl.CostEstimate(flops=cost, transcendentals=0, bytes_accessed=1024),
        name=name,
    )


def pick_kernel(me_ref, sel_ref, scale_ref, *refs):
    pieces, out_ref = refs[:-1], refs[-1]
    values = jnp.concatenate([p[...] for p in pieces], axis=0)
    out_ref[...] = (dot(sel_ref[...], values, 1, 0) * scale_ref[...]).astype(BF)


def forward_kernel(me_ref, x_ref, *refs):
    nb = (len(refs) - 5) // 2
    gates, ups = refs[:nb], refs[nb : 2 * nb]
    a_ref, b_ref, h_ref, gate_acc, up_acc = refs[2 * nb :]
    j = pl.program_id(1)
    x = x_ref[...].reshape(gate_acc.shape[0], x_ref.shape[-1])
    for s in range(nb):

        @pl.when(j == s)
        def _(s=s):
            for acc, w in ((gate_acc, gates[s]), (up_acc, ups[s])):
                part = dot(x, w[0], 1, 0)
                acc[...] = part if s == 0 else acc[...] + part

    @pl.when(j == nb - 1)
    def _():
        step = 64

        @pl.loop(0, gate_acc.shape[0] // step)
        def _(t):
            at = pl.ds(pl.multiple_of(t * step, step), step)
            gate, up = gate_acc[at, :], up_acc[at, :]
            sig = jax.nn.sigmoid(gate)
            act = gate * sig
            h_ref[0, at, :] = (act * up).astype(BF)
            a_ref[0, at, :] = up * sig * (1.0 + gate * (1.0 - sig))
            b_ref[0, at, :] = act


def outer_kernel(me_ref, x_ref, y_ref, *outs):
    j = pl.program_id(1)
    x = x_ref[...].reshape(y_ref.shape[1], x_ref.shape[-1])
    for s in range(len(outs)):

        @pl.when(j == s)
        def _(s=s):
            outs[s][0] = dot(x, y_ref[0], 0, 0).astype(BF)


def middle_kernel(me_ref, sg_ref, h_ref, a_ref, b_ref, *refs):
    nb = len(refs) - 4
    downs = refs[:nb]
    out_ref, gd_ref, ud_ref, acc = refs[nb:]
    j = pl.program_id(1)
    sg = sg_ref[...].reshape(acc.shape[0], sg_ref.shape[-1])
    for s in range(nb):

        @pl.when(j == s)
        def _(s=s):
            part = dot(sg, downs[s][0], 1, 0)
            acc[...] = part if s == 0 else acc[...] + part
            out_ref[...] = dot(h_ref[0], downs[s][0], 1, 1).astype(BF).reshape(out_ref.shape)

    @pl.when(j == nb - 1)
    def _():
        step = 64

        @pl.loop(0, acc.shape[0] // step)
        def _(t):
            at = pl.ds(pl.multiple_of(t * step, step), step)
            gh = acc[at, :]
            gd_ref[0, at, :] = (gh * a_ref[0, at, :]).astype(BF)
            ud_ref[0, at, :] = (gh * b_ref[0, at, :]).astype(BF)


def input_kernel(me_ref, gd_ref, ud_ref, *refs):
    nb = (len(refs) - 1) // 2
    gates, ups, out_ref = refs[:nb], refs[nb : 2 * nb], refs[-1]
    j = pl.program_id(1)
    for s in range(nb):

        @pl.when(j == s)
        def _(s=s):
            total = dot(gd_ref[0], gates[s][0], 1, 1) + dot(ud_ref[0], ups[s][0], 1, 1)
            out_ref[...] = total.astype(BF).reshape(out_ref.shape)


def expert_body(tokens, expert_ids, route_weight, gate_weight, up_weight, down_weight, out_grad):
    nb, ne = lax.axis_size("blk"), lax.axis_size("ep")
    me = lax.axis_index("blk")
    me_arr = me.reshape(1).astype(jnp.int32)
    tok, width = tokens.shape
    local_experts = gate_weight.shape[1]
    own = local_experts // nb
    chunk, inner = gate_weight.shape[0], gate_weight.shape[2]
    per = nb * CAP
    depth = ne * per
    slots = own * depth
    rows = nb * tok

    def hop(x, j):
        return lax.ppermute(x, "blk", [(i, i ^ j) for i in range(nb)])

    def after(x, *deps):
        return lax.optimization_barrier((x, deps))[0]

    def spread(x, deps=None):
        return [x] + [hop(x if deps is None else after(x, deps[j]), j) for j in range(1, nb)]

    def prepare(w):
        w = lax.optimization_barrier(jnp.swapaxes(w, 0, 1))
        return w, [lax.dynamic_slice_in_dim(w, (me ^ j) * own, own, 0) for j in range(1, nb)]

    def weight_pieces(prepared, deps):
        w, parts = prepared
        return [w] + [hop(after(parts[j - 1], deps[j]), j) for j in range(1, nb)]

    high = lax.reduce_precision(route_weight, 8, 7)
    mid = lax.reduce_precision(route_weight - high, 8, 7)
    low = route_weight - high - mid
    extra = jnp.concatenate([expert_ids.astype(F32), high, mid, low], axis=1).astype(BF)
    extra = jnp.pad(extra, ((0, 0), (0, 128 - extra.shape[1])))
    tok_p = spread(jnp.concatenate([tokens, extra], axis=1))
    gate_ready = prepare(gate_weight)
    tok_p, gate_ready = lax.optimization_barrier((tok_p, gate_ready))
    og_p = spread(out_grad)
    gate_p = weight_pieces(gate_ready, og_p)
    up_ready, down_ready = prepare(up_weight), prepare(down_weight)
    og_p, up_ready, down_ready = lax.optimization_barrier((og_p, up_ready, down_ready))
    extra = jnp.concatenate([p[:, width:] for p in tok_p], axis=0).astype(F32)
    top = expert_ids.shape[1]
    ids_all = extra[:, :top].astype(jnp.int32)
    rw_all = extra[:, top : 2 * top] + extra[:, 2 * top : 3 * top] + extra[:, 3 * top : 4 * top]

    row = jnp.arange(rows)
    before = ((row[:, None] > row[None, :]) & (row[:, None] // tok == row[None, :] // tok)).astype(BF)
    slot = jnp.arange(slots)
    slot_group, slot_rank = (slot // CAP) % nb, slot % CAP
    experts = (jnp.arange(ne)[:, None] * local_experts + me * own + jnp.arange(own)[None, :]).reshape(-1)
    eq = ids_all[:, :, None] == experts[None, None, :]
    member = jnp.any(eq, axis=1)
    weight = jnp.sum(jnp.where(eq, rw_all[:, :, None], 0.0), axis=1)
    rank = dot(before, member.astype(BF), 1, 0)
    rank = jnp.where(member, rank, -1.0).astype(jnp.int32)
    rank_s = jnp.repeat(rank.T, per, axis=0)
    weight_s = jnp.repeat(weight.T, per, axis=0)
    hit = (rank_s == slot_rank[:, None]) & (slot_group[:, None] == row[None, :] // tok)
    sel = hit.astype(BF)
    sel_w = jnp.where(hit, weight_s, 0.0)

    def pick(pieces, scale):
        tile = slots // 4
        return call(
            pick_kernel,
            "pick",
            (slots // tile,),
            [
                pl.BlockSpec((tile, rows), lambda t, m: (t, 0)),
                pl.BlockSpec((tile, 1), lambda t, m: (t, 0)),
            ]
            + [pl.BlockSpec((tok, width), lambda t, m: (0, 0))] * nb,
            pl.BlockSpec((tile, width), lambda t, m: (t, 0)),
            jax.ShapeDtypeStruct((slots, width), BF),
        )(me_arr, sel, scale, *pieces)

    previous = []

    def exchange(x):
        if previous:
            x, _ = lax.optimization_barrier((x, previous[-1]))
        x = x.reshape(ne, own * per, width)
        previous.append(lax.all_to_all(x, "ep", split_axis=0, concat_axis=0, tiled=True))
        return previous[-1].reshape(ne, own, per, width)

    routed = exchange(pick(tok_p, jnp.ones((slots, 1), F32)))
    slot_grad = pick(og_p, jnp.sum(sel_w, axis=1, keepdims=True))
    up_ready = after(up_ready, slot_grad)
    up_p = weight_pieces(up_ready, gate_p)
    down_p = weight_pieces(down_ready, up_p)
    graded = exchange(after(slot_grad, gate_p))

    grid = (own, nb)
    rows_spec = pl.BlockSpec((ne, None, per, chunk), lambda i, j, m: (0, i, 0, m[0] ^ j))
    wide_spec = pl.BlockSpec((1, depth, inner), lambda i, j, m: (i, 0, 0))
    piece_spec = pl.BlockSpec((1, chunk, inner), lambda i, j, m: (i, 0, 0))
    first_spec = pl.BlockSpec((1, chunk, inner), lambda i, j, m: (m[0] * own + i, 0, 0))
    weight_specs = [first_spec] + [piece_spec] * (nb - 1)
    wide = lambda dt: jax.ShapeDtypeStruct((own, depth, inner), dt)
    piece = jax.ShapeDtypeStruct((own, chunk, inner), BF)
    full = jax.ShapeDtypeStruct((ne, own, per, width), BF)
    acc = pltpu.VMEM((depth, inner), F32)

    a, b, hidden = call(
        forward_kernel,
        "forward",
        grid,
        [rows_spec] + weight_specs * 2,
        [wide_spec] * 3,
        [wide(F32), wide(F32), wide(BF)],
        [acc, acc],
    )(me_arr, routed, *gate_p, *up_p)

    def outer(x, y, cost):
        return call(
            outer_kernel,
            "outer",
            grid,
            [rows_spec, wide_spec],
            [piece_spec] * nb,
            [piece] * nb,
            (),
            cost,
        )(me_arr, x, y)

    def send_back(parts, deps):
        got = [parts[0]]
        for j in range(1, nb):
            got.append(hop(parts[j] if deps is None else after(parts[j], deps[j]), j))
        return got

    down_part = outer(graded, hidden, LIGHT)
    down_got = send_back(down_part, None)
    hidden = after(hidden, down_part)
    outs, gate_delta, up_delta = call(
        middle_kernel,
        "middle",
        grid,
        [rows_spec] + [wide_spec] * 3 + weight_specs,
        [rows_spec, wide_spec, wide_spec],
        [full, wide(BF), wide(BF)],
        [acc],
    )(me_arr, graded, hidden, a, b, *down_p)
    outs = exchange(outs).reshape(slots, width)
    gate_part = outer(routed, after(gate_delta, down_got), LIGHT)
    gate_part, up_delta = lax.optimization_barrier((gate_part, up_delta))
    up_part = outer(routed, up_delta, HEAVY)
    gate_got = send_back(gate_part, down_got)
    gate_delta = after(gate_delta, up_part)
    up_got = send_back(up_part, gate_got)
    backs = call(
        input_kernel,
        "inputs",
        grid,
        [wide_spec] * 2 + weight_specs * 2,
        rows_spec,
        full,
        (),
        HEAVY,
    )(me_arr, gate_delta, up_delta, *gate_p, *up_p)
    down_got = after(down_got, backs)
    backs = exchange(backs).reshape(slots, width)

    grad_down = finish(down_got, me, HEAVY)
    outs, grad_down = lax.optimization_barrier((outs, grad_down))
    high = lax.reduce_precision(sel_w, 8, 7)
    low = (sel_w - high).astype(BF)
    high = high.astype(BF)
    mixed = dot(high, outs, 0, 0) + dot(low, outs, 0, 0)
    score = dot(outs, jnp.concatenate(og_p, 0), 1, 1)
    score = jnp.where(hit, score, 0.0).reshape(ne * own, per, rows).sum(1)
    route_grad = jnp.sum(jnp.where(eq, score.T[:, None, :], 0.0), axis=2)
    grad_gate = finish(gate_got, me)
    def gather_back(x, deps=None):
        x = x.reshape((nb, tok) + x.shape[1:])
        total = x[0].astype(F32)
        for j in range(1, nb):
            part = x[j] if deps is None else after(x[j], deps[j])
            total += hop(part, j).astype(F32)
        return total

    mixed, grad_gate = lax.optimization_barrier((mixed, grad_gate))
    layer_output = gather_back(mixed.astype(BF), up_got).astype(BF)
    grad_route = gather_back(route_grad, up_got)
    backs, grad_down, grad_gate, layer_output, grad_route = lax.optimization_barrier(
        (backs, grad_down, grad_gate, layer_output, grad_route)
    )
    grad_tokens = gather_back(dot(sel, backs, 0, 0).astype(BF))
    return (
        layer_output,
        grad_tokens,
        grad_route,
        grad_gate,
        finish(up_got, me),
        grad_down,
    )


def finish_kernel(me_ref, *refs):
    nb = len(refs) - 3
    pieces, out_ref, wide, sems = refs[:nb], refs[nb], refs[nb + 1], refs[nb + 2]
    own = pieces[0].shape[0]
    copies = []
    for j in range(nb):
        for i in range(own):
            n = j * own + i
            wide[n] = pieces[j][i].astype(F32)
            place = (me_ref[0] ^ j) * own + i
            copies.append(pltpu.make_async_copy(wide.at[n], out_ref.at[:, place, :], sems.at[n]))
            copies[-1].start()
    for copy in copies:
        copy.wait()


def finish(pieces, me, cost=LIGHT):
    nb = len(pieces)
    own, chunk, inner = pieces[0].shape
    full = nb * own
    return call(
        finish_kernel,
        "finish",
        (1,),
        [pl.BlockSpec((own, chunk, inner), lambda t, m: (0, 0, 0))] * nb,
        pl.BlockSpec(memory_space=pl.ANY),
        jax.ShapeDtypeStruct((chunk, full, inner), F32),
        [pltpu.VMEM((full, chunk, inner), F32), pltpu.SemaphoreType.DMA((full,))],
        cost,
    )(me.reshape(1).astype(jnp.int32), *pieces)


def solution(mesh):
    in_specs = (
        P(("blk", "ep"), None),
        P(("blk", "ep"), None),
        P(("blk", "ep"), None),
        P("blk", "ep", None),
        P("blk", "ep", None),
        P("blk", "ep", None),
        P(("blk", "ep"), None),
    )
    out_specs = (
        P(("blk", "ep"), None),
        P(("blk", "ep"), None),
        P(("blk", "ep"), None),
        P("blk", "ep", None),
        P("blk", "ep", None),
        P("blk", "ep", None),
    )
    nb, ne = mesh.shape["blk"], mesh.shape["ep"]
    whole_experts = nb & (nb - 1) == 0 and (EXPERTS // ne) % nb == 0
    body = expert_body if whole_experts else gathered_body
    return jax.shard_map(body, mesh=mesh, in_specs=in_specs, out_specs=out_specs, check_vma=False)
```

```python
import jax
import jax.numpy as jnp
from jax import lax
from jax.experimental import pallas as pl
from jax.experimental.pallas import tpu as pltpu
from jax.sharding import PartitionSpec as P

EXPERTS = 64
CAP = 16
BF = jnp.bfloat16
F32 = jnp.float32


def dot(a, b, ca, cb):
    return lax.dot_general(a, b, (((ca,), (cb,)), ((), ())), preferred_element_type=F32)


def expand_rows(routed, weights):
    return jnp.einsum("erd,def->erf", routed, weights, preferred_element_type=jnp.float32)


def contract_rows(inner, weights):
    return jnp.einsum("erf,def->erd", inner, weights, preferred_element_type=jnp.float32)


def outer_rows(routed, inner):
    return jnp.einsum("erd,erf->def", routed, inner, preferred_element_type=jnp.float32)


def gathered_body(tokens, expert_ids, route_weight, gate_weight, up_weight, down_weight, out_grad):
    tok_count, model_width = tokens.shape
    top_count = expert_ids.shape[1]
    experts = EXPERTS
    capacity = CAP
    flat_ids = expert_ids.reshape(-1)
    onehot = (flat_ids[:, None] == jnp.arange(experts, dtype=jnp.int32)[None, :]).astype(jnp.int32)
    slot_rank = jnp.sum((jnp.cumsum(onehot, axis=0) - 1) * onehot, axis=1)
    target = flat_ids * capacity + slot_rank
    repeated = jnp.repeat(tokens, top_count, axis=0)
    outgoing = jnp.zeros((experts * capacity, model_width), jnp.bfloat16).at[target].set(repeated)
    received = lax.all_to_all(
        outgoing.reshape(experts, capacity, model_width),
        "ep",
        split_axis=0,
        concat_axis=1,
        tiled=True,
    )
    gate_full, up_full, down_full = (
        lax.all_gather(gate_weight, "blk", axis=0, tiled=True),
        lax.all_gather(up_weight, "blk", axis=0, tiled=True),
        lax.all_gather(down_weight, "blk", axis=0, tiled=True),
    )
    gate_pre = expand_rows(received, gate_full)
    up_pre = expand_rows(received, up_full)
    gate_sig = jax.nn.sigmoid(gate_pre)
    hidden = (gate_pre * gate_sig * up_pre).astype(jnp.bfloat16)
    expert_out = contract_rows(hidden, down_full).astype(jnp.bfloat16)
    returned = lax.all_to_all(expert_out, "ep", split_axis=1, concat_axis=0, tiled=True)
    chosen = returned.reshape(experts * capacity, model_width)[target].reshape(
        tok_count, top_count, model_width
    )
    chosen_f32 = chosen.astype(jnp.float32)
    layer_output = jnp.sum(route_weight[:, :, None] * chosen_f32, axis=1).astype(jnp.bfloat16)
    grad_f32 = out_grad.astype(jnp.float32)
    grad_route = jnp.sum(chosen_f32 * grad_f32[:, None, :], axis=2)
    slot_grad = (route_weight[:, :, None] * grad_f32[:, None, :]).astype(jnp.bfloat16)
    grad_send = (
        jnp.zeros((experts * capacity, model_width), jnp.bfloat16)
        .at[target]
        .set(slot_grad.reshape(-1, model_width))
    )
    grad_recv = lax.all_to_all(
        grad_send.reshape(experts, capacity, model_width),
        "ep",
        split_axis=0,
        concat_axis=1,
        tiled=True,
    )
    down_summed = lax.psum_scatter(
        outer_rows(grad_recv, hidden).astype(jnp.bfloat16), "blk", scatter_dimension=0, tiled=True
    ).astype(jnp.float32)
    grad_hidden = expand_rows(grad_recv, down_full)
    gate_delta = (grad_hidden * up_pre * gate_sig * (1.0 + gate_pre * (1.0 - gate_sig))).astype(
        jnp.bfloat16
    )
    up_delta = (grad_hidden * gate_pre * gate_sig).astype(jnp.bfloat16)
    input_grad = (contract_rows(gate_delta, gate_full) + contract_rows(up_delta, up_full)).astype(
        jnp.bfloat16
    )
    grad_back = lax.all_to_all(input_grad, "ep", split_axis=1, concat_axis=0, tiled=True)
    picked_grad = grad_back.reshape(experts * capacity, model_width)[target].reshape(
        tok_count, top_count, model_width
    )
    grad_tokens = jnp.sum(picked_grad.astype(jnp.float32), axis=1)
    pair_summed = lax.psum_scatter(
        jnp.stack(
            [outer_rows(received, gate_delta), outer_rows(received, up_delta)], axis=1
        ).astype(jnp.bfloat16),
        "blk",
        scatter_dimension=0,
        tiled=True,
    ).astype(jnp.float32)
    grad_gate = pair_summed[:, 0]
    grad_up = pair_summed[:, 1]
    return (layer_output, grad_tokens, grad_route, grad_gate, grad_up, down_summed)


LIGHT, HEAVY = 1 << 10, 1 << 37
COSTS = (1 << 34, 1 << 34, LIGHT, 1 << 35, HEAVY, LIGHT, 1 << 35, HEAVY)


def call(kernel, name, grid, in_specs, out_specs, out_shape, scratch=(), cost=LIGHT):
    return pl.pallas_call(
        kernel,
        grid_spec=pltpu.PrefetchScalarGridSpec(
            num_scalar_prefetch=1,
            grid=grid,
            in_specs=in_specs,
            out_specs=out_specs,
            scratch_shapes=scratch,
        ),
        out_shape=out_shape,
        compiler_params=pltpu.CompilerParams(vmem_limit_bytes=48 << 20),
        cost_estimate=pl.CostEstimate(flops=cost, transcendentals=0, bytes_accessed=1024),
        name=name,
    )


def pick_kernel(me_ref, sel_ref, scale_ref, *refs):
    pieces, out_ref = refs[:-1], refs[-1]
    values = jnp.concatenate([p[...] for p in pieces], axis=0)
    out_ref[...] = (dot(sel_ref[...], values, 1, 0) * scale_ref[...]).astype(BF)


def forward_kernel(me_ref, x_ref, *refs):
    nb = (len(refs) - 5) // 2
    gates, ups = refs[:nb], refs[nb : 2 * nb]
    a_ref, b_ref, h_ref, gate_acc, up_acc = refs[2 * nb :]
    j = pl.program_id(1)
    x = x_ref[...].reshape(gate_acc.shape[0], x_ref.shape[-1])
    for s in range(nb):

        @pl.when(j == s)
        def _(s=s):
            for acc, w in ((gate_acc, gates[s]), (up_acc, ups[s])):
                part = dot(x, w[0], 1, 0)
                acc[...] = part if s == 0 else acc[...] + part

    @pl.when(j == nb - 1)
    def _():
        step = 64

        @pl.loop(0, gate_acc.shape[0] // step)
        def _(t):
            at = pl.ds(pl.multiple_of(t * step, step), step)
            gate, up = gate_acc[at, :], up_acc[at, :]
            sig = jax.nn.sigmoid(gate)
            act = gate * sig
            h_ref[0, at, :] = (act * up).astype(BF)
            a_ref[0, at, :] = up * sig * (1.0 + gate * (1.0 - sig))
            b_ref[0, at, :] = act


def outer_kernel(me_ref, x_ref, y_ref, *outs):
    j = pl.program_id(1)
    x = x_ref[...].reshape(y_ref.shape[1], x_ref.shape[-1])
    for s in range(len(outs)):

        @pl.when(j == s)
        def _(s=s):
            outs[s][0] = dot(x, y_ref[0], 0, 0).astype(BF)


def output_kernel(me_ref, h_ref, *refs):
    downs, out_ref = refs[:-1], refs[-1]
    j = pl.program_id(1)
    for s in range(len(downs)):

        @pl.when(j == s)
        def _(s=s):
            out_ref[...] = dot(h_ref[0], downs[s][0], 1, 1).astype(BF).reshape(out_ref.shape)


def delta_kernel(me_ref, sg_ref, a_ref, b_ref, *refs):
    nb = len(refs) - 3
    downs = refs[:nb]
    gd_ref, ud_ref, acc = refs[nb:]
    j = pl.program_id(1)
    sg = sg_ref[...].reshape(acc.shape[0], sg_ref.shape[-1])
    for s in range(nb):

        @pl.when(j == s)
        def _(s=s):
            part = dot(sg, downs[s][0], 1, 0)
            acc[...] = part if s == 0 else acc[...] + part

    @pl.when(j == nb - 1)
    def _():
        step = 64

        @pl.loop(0, acc.shape[0] // step)
        def _(t):
            at = pl.ds(pl.multiple_of(t * step, step), step)
            gh = acc[at, :]
            gd_ref[0, at, :] = (gh * a_ref[0, at, :]).astype(BF)
            ud_ref[0, at, :] = (gh * b_ref[0, at, :]).astype(BF)


def input_kernel(me_ref, gd_ref, ud_ref, *refs):
    nb = (len(refs) - 1) // 2
    gates, ups, out_ref = refs[:nb], refs[nb : 2 * nb], refs[-1]
    j = pl.program_id(1)
    for s in range(nb):

        @pl.when(j == s)
        def _(s=s):
            total = dot(gd_ref[0], gates[s][0], 1, 1) + dot(ud_ref[0], ups[s][0], 1, 1)
            out_ref[...] = total.astype(BF).reshape(out_ref.shape)


def expert_body(tokens, expert_ids, route_weight, gate_weight, up_weight, down_weight, out_grad):
    nb, ne = lax.axis_size("blk"), lax.axis_size("ep")
    me = lax.axis_index("blk")
    me_arr = me.reshape(1).astype(jnp.int32)
    tok, width = tokens.shape
    local_experts = gate_weight.shape[1]
    own = local_experts // nb
    chunk, inner = gate_weight.shape[0], gate_weight.shape[2]
    per = nb * CAP
    depth = ne * per
    slots = own * depth
    rows = nb * tok

    def hop(x, j):
        return lax.ppermute(x, "blk", [(i, i ^ j) for i in range(nb)])

    def after(x, *deps):
        return lax.optimization_barrier((x, deps))[0]

    def spread(x, deps=None):
        return [x] + [hop(x if deps is None else after(x, deps[j]), j) for j in range(1, nb)]

    def prepare(w):
        w = lax.optimization_barrier(jnp.swapaxes(w, 0, 1))
        return w, [lax.dynamic_slice_in_dim(w, (me ^ j) * own, own, 0) for j in range(1, nb)]

    def weight_pieces(prepared, deps):
        w, parts = prepared
        return [w] + [hop(after(parts[j - 1], deps[j]), j) for j in range(1, nb)]

    high = lax.reduce_precision(route_weight, 8, 7)
    mid = lax.reduce_precision(route_weight - high, 8, 7)
    low = route_weight - high - mid
    extra = jnp.concatenate([expert_ids.astype(F32), high, mid, low], axis=1).astype(BF)
    extra = jnp.pad(extra, ((0, 0), (0, 128 - extra.shape[1])))
    tok_p = spread(jnp.concatenate([tokens, out_grad, extra], axis=1))
    gate_ready = prepare(gate_weight)
    tok_p, gate_ready = lax.optimization_barrier((tok_p, gate_ready))
    gate_p = weight_pieces(gate_ready, tok_p)
    up_ready, down_ready = prepare(up_weight), prepare(down_weight)
    extra = jnp.concatenate([p[:, 2 * width :] for p in tok_p], axis=0).astype(F32)
    top = expert_ids.shape[1]
    ids_all = extra[:, :top].astype(jnp.int32)
    rw_all = extra[:, top : 2 * top] + extra[:, 2 * top : 3 * top] + extra[:, 3 * top : 4 * top]

    row = jnp.arange(rows)
    before = ((row[:, None] > row[None, :]) & (row[:, None] // tok == row[None, :] // tok)).astype(BF)
    slot = jnp.arange(slots)
    slot_group, slot_rank = (slot // CAP) % nb, slot % CAP
    experts = (jnp.arange(ne)[:, None] * local_experts + me * own + jnp.arange(own)[None, :]).reshape(-1)
    eq = ids_all[:, :, None] == experts[None, None, :]
    member = jnp.any(eq, axis=1)
    weight = jnp.sum(jnp.where(eq, rw_all[:, :, None], 0.0), axis=1)
    rank = dot(before, member.astype(BF), 1, 0)
    rank = jnp.where(member, rank, -1.0).astype(jnp.int32)
    rank_s = jnp.repeat(rank.T, per, axis=0)
    weight_s = jnp.repeat(weight.T, per, axis=0)
    hit = (rank_s == slot_rank[:, None]) & (slot_group[:, None] == row[None, :] // tok)
    sel = hit.astype(BF)
    sel_w = jnp.where(hit, weight_s, 0.0)

    def pick(pieces, scale, half, cost):
        tile = slots // 4
        return call(
            pick_kernel,
            "pick",
            (slots // tile,),
            [
                pl.BlockSpec((tile, rows), lambda t, m: (t, 0)),
                pl.BlockSpec((tile, 1), lambda t, m: (t, 0)),
            ]
            + [pl.BlockSpec((tok, width), lambda t, m: (0, half))] * nb,
            pl.BlockSpec((tile, width), lambda t, m: (t, 0)),
            jax.ShapeDtypeStruct((slots, width), BF),
            (),
            cost,
        )(me_arr, sel, scale, *pieces)

    previous = []

    def exchange(x):
        if previous:
            x, _ = lax.optimization_barrier((x, previous[-1]))
        x = x.reshape(ne, own * per, width)
        previous.append(lax.all_to_all(x, "ep", split_axis=0, concat_axis=0, tiled=True))
        return previous[-1].reshape(ne, own, per, width)

    routed = exchange(pick(tok_p, jnp.ones((slots, 1), F32), 0, LIGHT))
    scale = jnp.sum(sel_w, axis=1, keepdims=True)
    late_p, scale, up_ready, down_ready = lax.optimization_barrier((tok_p, scale, up_ready, down_ready))
    slot_grad = pick(after(late_p, gate_p), scale, 1, COSTS[7])
    up_p = weight_pieces(up_ready, gate_p)
    down_p = weight_pieces(down_ready, up_p)
    graded = exchange(after(slot_grad, gate_p))

    grid = (own, nb)
    rows_spec = pl.BlockSpec((ne, None, per, chunk), lambda i, j, m: (0, i, 0, m[0] ^ j))
    wide_spec = pl.BlockSpec((1, depth, inner), lambda i, j, m: (i, 0, 0))
    piece_spec = pl.BlockSpec((1, chunk, inner), lambda i, j, m: (i, 0, 0))
    first_spec = pl.BlockSpec((1, chunk, inner), lambda i, j, m: (m[0] * own + i, 0, 0))
    weight_specs = [first_spec] + [piece_spec] * (nb - 1)
    wide = lambda dt: jax.ShapeDtypeStruct((own, depth, inner), dt)
    piece = jax.ShapeDtypeStruct((own, chunk, inner), BF)
    full = jax.ShapeDtypeStruct((ne, own, per, width), BF)
    acc = pltpu.VMEM((depth, inner), F32)

    a, b, hidden = call(
        forward_kernel,
        "forward",
        grid,
        [rows_spec] + weight_specs * 2,
        [wide_spec] * 3,
        [wide(F32), wide(F32), wide(BF)],
        [acc, acc],
        COSTS[6],
    )(me_arr, routed, *gate_p, *up_p)

    def outer(x, y, cost):
        return call(
            outer_kernel,
            "outer",
            grid,
            [rows_spec, wide_spec],
            [piece_spec] * nb,
            [piece] * nb,
            (),
            cost,
        )(me_arr, x, y)

    def send_back(parts, deps):
        got = [parts[0]]
        for j in range(1, nb):
            got.append(hop(parts[j] if deps is None else after(parts[j], deps[j]), j))
        return got

    outs = call(
        output_kernel, "outputs", grid, [wide_spec] + weight_specs, rows_spec, full
    )(me_arr, hidden, *down_p)
    graded, outs = lax.optimization_barrier((graded, outs))
    down_part = outer(graded, hidden, LIGHT)
    down_got = send_back(down_part, None)
    graded = after(graded, down_part)
    gate_delta, up_delta = call(
        delta_kernel,
        "deltas",
        grid,
        [rows_spec] + [wide_spec] * 2 + weight_specs,
        [wide_spec] * 2,
        [wide(BF), wide(BF)],
        [acc],
        COSTS[0],
    )(me_arr, graded, a, b, *down_p)
    outs = exchange(after(outs, down_part)).reshape(slots, width)
    gate_part = outer(routed, gate_delta, COSTS[1])
    gate_got = send_back(gate_part, down_got)
    gate_delta = after(gate_delta, gate_part)
    backs = call(
        input_kernel,
        "inputs",
        grid,
        [wide_spec] * 2 + weight_specs * 2,
        rows_spec,
        full,
        (),
        COSTS[3],
    )(me_arr, gate_delta, up_delta, *gate_p, *up_p)
    up_part = outer(routed, after(up_delta, backs), COSTS[2])
    up_got = send_back(up_part, gate_got)
    down_got = after(down_got, backs)
    backs = exchange(backs).reshape(slots, width)

    grad_down = finish(down_got, me, COSTS[4])
    outs, grad_down = lax.optimization_barrier((outs, grad_down))
    high = lax.reduce_precision(sel_w, 8, 7)
    low = (sel_w - high).astype(BF)
    high = high.astype(BF)
    mixed = dot(high, outs, 0, 0) + dot(low, outs, 0, 0)
    score = dot(outs, jnp.concatenate([p[:, width : 2 * width] for p in tok_p], 0), 1, 1)
    score = jnp.where(hit, score, 0.0).reshape(ne * own, per, rows).sum(1)
    route_grad = jnp.sum(jnp.where(eq, score.T[:, None, :], 0.0), axis=2)
    grad_gate = finish(gate_got, me, COSTS[5])
    def gather_back(x, deps=None):
        x = x.reshape((nb, tok) + x.shape[1:])
        total = x[0].astype(F32)
        for j in range(1, nb):
            part = x[j] if deps is None else after(x[j], deps[j])
            total += hop(part, j).astype(F32)
        return total

    route_high = lax.reduce_precision(route_grad, 8, 7)
    route_mid = lax.reduce_precision(route_grad - route_high, 8, 7)
    route_low = route_grad - route_high - route_mid
    route_all = jnp.concatenate([route_high, route_mid, route_low], axis=1)
    route_all = jnp.pad(route_all, ((0, 0), (0, 128 - route_all.shape[1])))
    payload = jnp.concatenate([mixed, route_all], axis=1).astype(BF)
    payload, grad_gate, grad_down, backs = lax.optimization_barrier((payload, grad_gate, grad_down, backs))
    layer_sum = gather_back(payload, up_got)
    layer_output = layer_sum[:, :width].astype(BF)
    route_sum = layer_sum[:, width:]
    grad_route = route_sum[:, :top] + route_sum[:, top : 2 * top] + route_sum[:, 2 * top : 3 * top]
    grad_tokens = gather_back(dot(sel, backs, 0, 0).astype(BF))
    return (
        layer_output,
        grad_tokens,
        grad_route,
        grad_gate,
        finish(up_got, me),
        grad_down,
    )


def finish_kernel(me_ref, *refs):
    nb = len(refs) - 3
    pieces, out_ref, wide, sems = refs[:nb], refs[nb], refs[nb + 1], refs[nb + 2]
    own = pieces[0].shape[0]
    copies = []
    for j in range(nb):
        for i in range(own):
            n = j * own + i
            wide[n] = pieces[j][i].astype(F32)
            place = (me_ref[0] ^ j) * own + i
            copies.append(pltpu.make_async_copy(wide.at[n], out_ref.at[:, place, :], sems.at[n]))
            copies[-1].start()
    for copy in copies:
        copy.wait()


def finish(pieces, me, cost=LIGHT):
    nb = len(pieces)
    own, chunk, inner = pieces[0].shape
    full = nb * own
    return call(
        finish_kernel,
        "finish",
        (1,),
        [pl.BlockSpec((own, chunk, inner), lambda t, m: (0, 0, 0))] * nb,
        pl.BlockSpec(memory_space=pl.ANY),
        jax.ShapeDtypeStruct((chunk, full, inner), F32),
        [pltpu.VMEM((full, chunk, inner), F32), pltpu.SemaphoreType.DMA((full,))],
        cost,
    )(me.reshape(1).astype(jnp.int32), *pieces)


def solution(mesh):
    in_specs = (
        P(("blk", "ep"), None),
        P(("blk", "ep"), None),
        P(("blk", "ep"), None),
        P("blk", "ep", None),
        P("blk", "ep", None),
        P("blk", "ep", None),
        P(("blk", "ep"), None),
    )
    out_specs = (
        P(("blk", "ep"), None),
        P(("blk", "ep"), None),
        P(("blk", "ep"), None),
        P("blk", "ep", None),
        P("blk", "ep", None),
        P("blk", "ep", None),
    )
    nb, ne = mesh.shape["blk"], mesh.shape["ep"]
    whole_experts = nb & (nb - 1) == 0 and (EXPERTS // ne) % nb == 0
    body = expert_body if whole_experts else gathered_body
    return jax.shard_map(body, mesh=mesh, in_specs=in_specs, out_specs=out_specs, check_vma=False)
```

```python
import functools

import jax
import jax.numpy as jnp
from jax import lax
from jax.experimental import pallas as pl
from jax.experimental.pallas import tpu as pltpu
from jax.sharding import PartitionSpec as P

EXPERTS = 64
CAP = 16
BF = jnp.bfloat16
F32 = jnp.float32


def dot(a, b, ca, cb):
    return lax.dot_general(a, b, (((ca,), (cb,)), ((), ())), preferred_element_type=F32)


def expand_rows(routed, weights):
    return jnp.einsum("erd,def->erf", routed, weights, preferred_element_type=jnp.float32)


def contract_rows(inner, weights):
    return jnp.einsum("erf,def->erd", inner, weights, preferred_element_type=jnp.float32)


def outer_rows(routed, inner):
    return jnp.einsum("erd,erf->def", routed, inner, preferred_element_type=jnp.float32)


def gathered_body(tokens, expert_ids, route_weight, gate_weight, up_weight, down_weight, out_grad):
    tok_count, model_width = tokens.shape
    top_count = expert_ids.shape[1]
    experts = EXPERTS
    capacity = CAP
    flat_ids = expert_ids.reshape(-1)
    onehot = (flat_ids[:, None] == jnp.arange(experts, dtype=jnp.int32)[None, :]).astype(jnp.int32)
    slot_rank = jnp.sum((jnp.cumsum(onehot, axis=0) - 1) * onehot, axis=1)
    target = flat_ids * capacity + slot_rank
    repeated = jnp.repeat(tokens, top_count, axis=0)
    outgoing = jnp.zeros((experts * capacity, model_width), jnp.bfloat16).at[target].set(repeated)
    received = lax.all_to_all(
        outgoing.reshape(experts, capacity, model_width),
        "ep",
        split_axis=0,
        concat_axis=1,
        tiled=True,
    )
    gate_full, up_full, down_full = (
        lax.all_gather(gate_weight, "blk", axis=0, tiled=True),
        lax.all_gather(up_weight, "blk", axis=0, tiled=True),
        lax.all_gather(down_weight, "blk", axis=0, tiled=True),
    )
    gate_pre = expand_rows(received, gate_full)
    up_pre = expand_rows(received, up_full)
    gate_sig = jax.nn.sigmoid(gate_pre)
    hidden = (gate_pre * gate_sig * up_pre).astype(jnp.bfloat16)
    expert_out = contract_rows(hidden, down_full).astype(jnp.bfloat16)
    returned = lax.all_to_all(expert_out, "ep", split_axis=1, concat_axis=0, tiled=True)
    chosen = returned.reshape(experts * capacity, model_width)[target].reshape(
        tok_count, top_count, model_width
    )
    chosen_f32 = chosen.astype(jnp.float32)
    layer_output = jnp.sum(route_weight[:, :, None] * chosen_f32, axis=1).astype(jnp.bfloat16)
    grad_f32 = out_grad.astype(jnp.float32)
    grad_route = jnp.sum(chosen_f32 * grad_f32[:, None, :], axis=2)
    slot_grad = (route_weight[:, :, None] * grad_f32[:, None, :]).astype(jnp.bfloat16)
    grad_send = (
        jnp.zeros((experts * capacity, model_width), jnp.bfloat16)
        .at[target]
        .set(slot_grad.reshape(-1, model_width))
    )
    grad_recv = lax.all_to_all(
        grad_send.reshape(experts, capacity, model_width),
        "ep",
        split_axis=0,
        concat_axis=1,
        tiled=True,
    )
    down_summed = lax.psum_scatter(
        outer_rows(grad_recv, hidden).astype(jnp.bfloat16), "blk", scatter_dimension=0, tiled=True
    ).astype(jnp.float32)
    grad_hidden = expand_rows(grad_recv, down_full)
    gate_delta = (grad_hidden * up_pre * gate_sig * (1.0 + gate_pre * (1.0 - gate_sig))).astype(
        jnp.bfloat16
    )
    up_delta = (grad_hidden * gate_pre * gate_sig).astype(jnp.bfloat16)
    input_grad = (contract_rows(gate_delta, gate_full) + contract_rows(up_delta, up_full)).astype(
        jnp.bfloat16
    )
    grad_back = lax.all_to_all(input_grad, "ep", split_axis=1, concat_axis=0, tiled=True)
    picked_grad = grad_back.reshape(experts * capacity, model_width)[target].reshape(
        tok_count, top_count, model_width
    )
    grad_tokens = jnp.sum(picked_grad.astype(jnp.float32), axis=1)
    pair_summed = lax.psum_scatter(
        jnp.stack(
            [outer_rows(received, gate_delta), outer_rows(received, up_delta)], axis=1
        ).astype(jnp.bfloat16),
        "blk",
        scatter_dimension=0,
        tiled=True,
    ).astype(jnp.float32)
    grad_gate = pair_summed[:, 0]
    grad_up = pair_summed[:, 1]
    return (layer_output, grad_tokens, grad_route, grad_gate, grad_up, down_summed)


LIGHT, HEAVY = 1 << 10, 1 << 37
COSTS = (1 << 34, 1 << 34, LIGHT, 1 << 35, HEAVY, LIGHT, 1 << 35, HEAVY)


def call(kernel, name, grid, in_specs, out_specs, out_shape, scratch=(), cost=LIGHT):
    return pl.pallas_call(
        kernel,
        grid_spec=pltpu.PrefetchScalarGridSpec(
            num_scalar_prefetch=1,
            grid=grid,
            in_specs=in_specs,
            out_specs=out_specs,
            scratch_shapes=scratch,
        ),
        out_shape=out_shape,
        compiler_params=pltpu.CompilerParams(vmem_limit_bytes=48 << 20),
        cost_estimate=pl.CostEstimate(flops=cost, transcendentals=0, bytes_accessed=1024),
        name=name,
    )


def pick_kernel(me_ref, sel_ref, scale_ref, *refs):
    pieces, out_ref = refs[:-1], refs[-1]
    values = jnp.concatenate([p[...] for p in pieces], axis=0)
    out_ref[...] = (dot(sel_ref[...], values, 1, 0) * scale_ref[...]).astype(BF)


def forward_kernel(me_ref, x_ref, *refs):
    nb = (len(refs) - 5) // 2
    gates, ups = refs[:nb], refs[nb : 2 * nb]
    a_ref, b_ref, h_ref, gate_acc, up_acc = refs[2 * nb :]
    j = pl.program_id(1)
    x = x_ref[...].reshape(gate_acc.shape[0], x_ref.shape[-1])
    for s in range(nb):

        @pl.when(j == s)
        def _(s=s):
            for acc, w in ((gate_acc, gates[s]), (up_acc, ups[s])):
                part = dot(x, w[0], 1, 0)
                acc[...] = part if s == 0 else acc[...] + part

    @pl.when(j == nb - 1)
    def _():
        step = 64

        @pl.loop(0, gate_acc.shape[0] // step)
        def _(t):
            at = pl.ds(pl.multiple_of(t * step, step), step)
            gate, up = gate_acc[at, :], up_acc[at, :]
            sig = jax.nn.sigmoid(gate)
            act = gate * sig
            h_ref[0, at, :] = (act * up).astype(BF)
            a_ref[0, at, :] = up * sig * (1.0 + gate * (1.0 - sig))
            b_ref[0, at, :] = act


def outer_kernel(count, me_ref, x_ref, *refs):
    ys, outs = refs[:count], refs[count:]
    nb = len(outs) // count
    j = pl.program_id(1)
    x = x_ref[...].reshape(ys[0].shape[1], x_ref.shape[-1])
    for s in range(nb):

        @pl.when(j == s)
        def _(s=s):
            for n in range(count):
                outs[n * nb + s][0] = dot(x, ys[n][0], 0, 0).astype(BF)


def output_kernel(me_ref, h_ref, *refs):
    downs, out_ref = refs[:-1], refs[-1]
    j = pl.program_id(1)
    for s in range(len(downs)):

        @pl.when(j == s)
        def _(s=s):
            out_ref[...] = dot(h_ref[0], downs[s][0], 1, 1).astype(BF).reshape(out_ref.shape)


def delta_kernel(me_ref, sg_ref, a_ref, b_ref, *refs):
    nb = len(refs) - 3
    downs = refs[:nb]
    gd_ref, ud_ref, acc = refs[nb:]
    j = pl.program_id(1)
    sg = sg_ref[...].reshape(acc.shape[0], sg_ref.shape[-1])
    for s in range(nb):

        @pl.when(j == s)
        def _(s=s):
            part = dot(sg, downs[s][0], 1, 0)
            acc[...] = part if s == 0 else acc[...] + part

    @pl.when(j == nb - 1)
    def _():
        step = 64

        @pl.loop(0, acc.shape[0] // step)
        def _(t):
            at = pl.ds(pl.multiple_of(t * step, step), step)
            gh = acc[at, :]
            gd_ref[0, at, :] = (gh * a_ref[0, at, :]).astype(BF)
            ud_ref[0, at, :] = (gh * b_ref[0, at, :]).astype(BF)


def input_kernel(me_ref, gd_ref, ud_ref, *refs):
    nb = (len(refs) - 1) // 2
    gates, ups, out_ref = refs[:nb], refs[nb : 2 * nb], refs[-1]
    j = pl.program_id(1)
    for s in range(nb):

        @pl.when(j == s)
        def _(s=s):
            total = dot(gd_ref[0], gates[s][0], 1, 1) + dot(ud_ref[0], ups[s][0], 1, 1)
            out_ref[...] = total.astype(BF).reshape(out_ref.shape)


def expert_body(tokens, expert_ids, route_weight, gate_weight, up_weight, down_weight, out_grad):
    nb, ne = lax.axis_size("blk"), lax.axis_size("ep")
    me = lax.axis_index("blk")
    me_arr = me.reshape(1).astype(jnp.int32)
    tok, width = tokens.shape
    local_experts = gate_weight.shape[1]
    own = local_experts // nb
    chunk, inner = gate_weight.shape[0], gate_weight.shape[2]
    per = nb * CAP
    depth = ne * per
    slots = own * depth
    rows = nb * tok

    def hop(x, j):
        return lax.ppermute(x, "blk", [(i, i ^ j) for i in range(nb)])

    def after(x, *deps):
        return lax.optimization_barrier((x, deps))[0]

    def spread(x, deps=None):
        return [x] + [hop(x if deps is None else after(x, deps[j]), j) for j in range(1, nb)]

    def prepare(w):
        w = lax.optimization_barrier(jnp.swapaxes(w, 0, 1))
        return w, [lax.dynamic_slice_in_dim(w, (me ^ j) * own, own, 0) for j in range(1, nb)]

    def weight_pieces(prepared, deps):
        w, parts = prepared
        return [w] + [hop(after(parts[j - 1], deps[j]), j) for j in range(1, nb)]

    high = lax.reduce_precision(route_weight, 8, 7)
    mid = lax.reduce_precision(route_weight - high, 8, 7)
    low = route_weight - high - mid
    extra = jnp.concatenate([expert_ids.astype(F32), high, mid, low], axis=1).astype(BF)
    extra = jnp.pad(extra, ((0, 0), (0, 128 - extra.shape[1])))
    tok_p = spread(jnp.concatenate([tokens, out_grad, extra], axis=1))
    gate_ready = prepare(gate_weight)
    tok_p, gate_ready = lax.optimization_barrier((tok_p, gate_ready))
    gate_p = weight_pieces(gate_ready, tok_p)
    up_ready, down_ready = prepare(up_weight), prepare(down_weight)
    extra = jnp.concatenate([p[:, 2 * width :] for p in tok_p], axis=0).astype(F32)
    top = expert_ids.shape[1]
    ids_all = extra[:, :top].astype(jnp.int32)
    rw_all = extra[:, top : 2 * top] + extra[:, 2 * top : 3 * top] + extra[:, 3 * top : 4 * top]

    row = jnp.arange(rows)
    before = ((row[:, None] > row[None, :]) & (row[:, None] // tok == row[None, :] // tok)).astype(BF)
    slot = jnp.arange(slots)
    slot_group, slot_rank = (slot // CAP) % nb, slot % CAP
    experts = (jnp.arange(ne)[:, None] * local_experts + me * own + jnp.arange(own)[None, :]).reshape(-1)
    eq = ids_all[:, :, None] == experts[None, None, :]
    member = jnp.any(eq, axis=1)
    weight = jnp.sum(jnp.where(eq, rw_all[:, :, None], 0.0), axis=1)
    rank = dot(before, member.astype(BF), 1, 0)
    rank = jnp.where(member, rank, -1.0).astype(jnp.int32)
    rank_s = jnp.repeat(rank.T, per, axis=0)
    weight_s = jnp.repeat(weight.T, per, axis=0)
    hit = (rank_s == slot_rank[:, None]) & (slot_group[:, None] == row[None, :] // tok)
    sel = hit.astype(BF)
    sel_w = jnp.where(hit, weight_s, 0.0)

    def pick(pieces, scale, half, cost):
        tile = slots // 4
        return call(
            pick_kernel,
            "pick",
            (slots // tile,),
            [
                pl.BlockSpec((tile, rows), lambda t, m: (t, 0)),
                pl.BlockSpec((tile, 1), lambda t, m: (t, 0)),
            ]
            + [pl.BlockSpec((tok, width), lambda t, m: (0, half))] * nb,
            pl.BlockSpec((tile, width), lambda t, m: (t, 0)),
            jax.ShapeDtypeStruct((slots, width), BF),
            (),
            cost,
        )(me_arr, sel, scale, *pieces)

    previous = []

    def exchange(x):
        if previous:
            x, _ = lax.optimization_barrier((x, previous[-1]))
        x = x.reshape(ne, own * per, width)
        previous.append(lax.all_to_all(x, "ep", split_axis=0, concat_axis=0, tiled=True))
        return previous[-1].reshape(ne, own, per, width)

    routed = exchange(pick(tok_p, jnp.ones((slots, 1), F32), 0, LIGHT))
    scale = jnp.sum(sel_w, axis=1, keepdims=True)
    late_p, scale, up_ready, down_ready = lax.optimization_barrier((tok_p, scale, up_ready, down_ready))
    slot_grad = pick(after(late_p, gate_p), scale, 1, COSTS[7])
    up_p = weight_pieces(up_ready, gate_p)
    down_p = weight_pieces(down_ready, up_p)
    graded = exchange(after(slot_grad, gate_p))

    grid = (own, nb)
    rows_spec = pl.BlockSpec((ne, None, per, chunk), lambda i, j, m: (0, i, 0, m[0] ^ j))
    wide_spec = pl.BlockSpec((1, depth, inner), lambda i, j, m: (i, 0, 0))
    piece_spec = pl.BlockSpec((1, chunk, inner), lambda i, j, m: (i, 0, 0))
    first_spec = pl.BlockSpec((1, chunk, inner), lambda i, j, m: (m[0] * own + i, 0, 0))
    weight_specs = [first_spec] + [piece_spec] * (nb - 1)
    wide = lambda dt: jax.ShapeDtypeStruct((own, depth, inner), dt)
    piece = jax.ShapeDtypeStruct((own, chunk, inner), BF)
    full = jax.ShapeDtypeStruct((ne, own, per, width), BF)
    acc = pltpu.VMEM((depth, inner), F32)

    a, b, hidden = call(
        forward_kernel,
        "forward",
        grid,
        [rows_spec] + weight_specs * 2,
        [wide_spec] * 3,
        [wide(F32), wide(F32), wide(BF)],
        [acc, acc],
        COSTS[6],
    )(me_arr, routed, *gate_p, *up_p)

    def outer(x, ys, cost):
        count = len(ys)
        got = call(
            functools.partial(outer_kernel, count),
            "outer",
            grid,
            [rows_spec] + [wide_spec] * count,
            [piece_spec] * (nb * count),
            [piece] * (nb * count),
            (),
            cost,
        )(me_arr, x, *ys)
        return [got[n * nb : (n + 1) * nb] for n in range(count)]

    def send_back(parts, deps):
        got = [parts[0]]
        for j in range(1, nb):
            got.append(hop(parts[j] if deps is None else after(parts[j], deps[j]), j))
        return got

    outs = call(
        output_kernel, "outputs", grid, [wide_spec] + weight_specs, rows_spec, full
    )(me_arr, hidden, *down_p)
    graded, outs = lax.optimization_barrier((graded, outs))
    (down_part,) = outer(graded, [hidden], LIGHT)
    down_got = send_back(down_part, None)
    graded = after(graded, down_part)
    gate_delta, up_delta = call(
        delta_kernel,
        "deltas",
        grid,
        [rows_spec] + [wide_spec] * 2 + weight_specs,
        [wide_spec] * 2,
        [wide(BF), wide(BF)],
        [acc],
        COSTS[0],
    )(me_arr, graded, a, b, *down_p)
    outs = exchange(after(outs, down_part)).reshape(slots, width)
    gate_part, up_part = outer(routed, [gate_delta, up_delta], COSTS[1])
    gate_got = send_back(gate_part, down_got)
    gate_delta = after(gate_delta, gate_part)
    backs = call(
        input_kernel,
        "inputs",
        grid,
        [wide_spec] * 2 + weight_specs * 2,
        rows_spec,
        full,
        (),
        COSTS[3],
    )(me_arr, gate_delta, up_delta, *gate_p, *up_p)
    up_got = send_back(up_part, gate_got)
    down_got = after(down_got, backs)
    backs = exchange(backs).reshape(slots, width)

    grad_down = finish(down_got, me, COSTS[4])
    outs, grad_down = lax.optimization_barrier((outs, grad_down))
    high = lax.reduce_precision(sel_w, 8, 7)
    low = (sel_w - high).astype(BF)
    high = high.astype(BF)
    mixed = dot(high, outs, 0, 0) + dot(low, outs, 0, 0)
    score = dot(outs, jnp.concatenate([p[:, width : 2 * width] for p in tok_p], 0), 1, 1)
    score = jnp.where(hit, score, 0.0).reshape(ne * own, per, rows).sum(1)
    route_grad = jnp.sum(jnp.where(eq, score.T[:, None, :], 0.0), axis=2)
    grad_gate = finish(gate_got, me, COSTS[5])
    def gather_back(x, deps=None):
        x = x.reshape((nb, tok) + x.shape[1:])
        total = x[0].astype(F32)
        for j in range(1, nb):
            part = x[j] if deps is None else after(x[j], deps[j])
            total += hop(part, j).astype(F32)
        return total

    route_high = lax.reduce_precision(route_grad, 8, 7)
    route_mid = lax.reduce_precision(route_grad - route_high, 8, 7)
    route_low = route_grad - route_high - route_mid
    route_all = jnp.concatenate([route_high, route_mid, route_low], axis=1)
    route_all = jnp.pad(route_all, ((0, 0), (0, 128 - route_all.shape[1])))
    payload = jnp.concatenate([mixed, route_all], axis=1).astype(BF)
    payload, grad_gate, grad_down, backs = lax.optimization_barrier((payload, grad_gate, grad_down, backs))
    layer_sum = gather_back(payload, up_got)
    layer_output = layer_sum[:, :width].astype(BF)
    route_sum = layer_sum[:, width:]
    grad_route = route_sum[:, :top] + route_sum[:, top : 2 * top] + route_sum[:, 2 * top : 3 * top]
    grad_tokens = gather_back(dot(sel, backs, 0, 0).astype(BF))
    return (
        layer_output,
        grad_tokens,
        grad_route,
        grad_gate,
        finish(up_got, me),
        grad_down,
    )


def finish_kernel(me_ref, *refs):
    nb = len(refs) - 3
    pieces, out_ref, wide, sems = refs[:nb], refs[nb], refs[nb + 1], refs[nb + 2]
    own = pieces[0].shape[0]
    copies = []
    for j in range(nb):
        for i in range(own):
            n = j * own + i
            wide[n] = pieces[j][i].astype(F32)
            place = (me_ref[0] ^ j) * own + i
            copies.append(pltpu.make_async_copy(wide.at[n], out_ref.at[:, place, :], sems.at[n]))
            copies[-1].start()
    for copy in copies:
        copy.wait()


def finish(pieces, me, cost=LIGHT):
    nb = len(pieces)
    own, chunk, inner = pieces[0].shape
    full = nb * own
    return call(
        finish_kernel,
        "finish",
        (1,),
        [pl.BlockSpec((own, chunk, inner), lambda t, m: (0, 0, 0))] * nb,
        pl.BlockSpec(memory_space=pl.ANY),
        jax.ShapeDtypeStruct((chunk, full, inner), F32),
        [pltpu.VMEM((full, chunk, inner), F32), pltpu.SemaphoreType.DMA((full,))],
        cost,
    )(me.reshape(1).astype(jnp.int32), *pieces)


def solution(mesh):
    in_specs = (
        P(("blk", "ep"), None),
        P(("blk", "ep"), None),
        P(("blk", "ep"), None),
        P("blk", "ep", None),
        P("blk", "ep", None),
        P("blk", "ep", None),
        P(("blk", "ep"), None),
    )
    out_specs = (
        P(("blk", "ep"), None),
        P(("blk", "ep"), None),
        P(("blk", "ep"), None),
        P("blk", "ep", None),
        P("blk", "ep", None),
        P("blk", "ep", None),
    )
    nb, ne = mesh.shape["blk"], mesh.shape["ep"]
    whole_experts = nb & (nb - 1) == 0 and (EXPERTS // ne) % nb == 0
    body = expert_body if whole_experts else gathered_body
    return jax.shard_map(body, mesh=mesh, in_specs=in_specs, out_specs=out_specs, check_vma=False)
```
